32 devices in a mesh: dp: 8 (over y, x, core), tensor: 4 (over z).
Axes of the slice: x: 2, y: 2, z: 4, core: 2. Of those that a mesh axis runs over, the one named last changes fastest.
Arguments:
- wq_flat: bfloat16 [8192, 4096], P(('dp', 'tensor')), may hold values from -0.125 to 0.125
- hidden: bfloat16 [4, 16, 8192], P(None, 'dp'), may hold values from -6 to 6
- cache: bfloat16 [16, 4, 8192, 256], P('dp', None, 'tensor'), may hold values from -300 to 300
- new_kv: bfloat16 [4, 16, 4, 256], P(None, 'dp'), may hold values from -6 to 6
- lengths: int32 [16], P('dp'), may hold values from 1 to 8192, as said below
Outputs:
- attended: bfloat16 [4, 16, 4096], P(None, 'dp', 'tensor')
The draws below stay inside these ranges and needn't reach their ends.
Inputs may be any that keep to these rules, and one draw needn't show every extreme that they name: `lengths`: every sequence has at least one cached position; in every draw some sequence has exactly 8192.
All inputs are finite; a program needn't handle non-finite values.
Results may differ from the reference program's by a relative error of at most 0.03.
Values may be sent and summed in bfloat16 or wider, within the bound.
A program may use at most 64 MiB of HBM per device.

```python
import jax
import jax.numpy as jnp
from jax import lax

D = 8192
QH = 32
KVH = 4
HD = 128
STEPS = 4
CTX = 8192
QW = 4096
SEQS = 16


def draw_cache(key, part):
    base = jnp.clip(jax.random.normal(key, (SEQS, KVH, CTX, 2 * HD), jnp.float32), -6.0, 6.0)
    factor = jnp.full((SEQS, KVH, CTX, 1), 3.0, jnp.float32)
    base = jnp.concatenate([base[..., :HD] * factor, base[..., HD:]], axis=-1)
    return base.astype(jnp.bfloat16)


def draw_lengths(key, part):
    key_len = jax.random.fold_in(key, 21)
    key_pick = jax.random.fold_in(key, 22)
    spans = jax.random.randint(key_len, (SEQS,), 1, CTX + 1)
    chosen = jax.random.randint(key_pick, (), 0, SEQS)
    return jnp.where(jnp.arange(SEQS) == chosen, CTX, spans).astype(jnp.int32)


def raised(values, key, source, target, parts, factor):
    def block_of(dim):
        return (jnp.arange(values.shape[dim]) // (values.shape[dim] // parts)).reshape((-1,) + (1,) * (values.ndim - 1 - dim))

    first = jax.random.permutation(key, parts)[block_of(target)]
    second = (block_of(target) + parts // 2) % parts
    return jnp.where((block_of(source) == first) | (block_of(source) == second), factor * values, values)


def block_scale(rng, dims, shards, low, largest):
    loudness = 1.0
    for axis_at, blocks in shards:
        draws = jax.random.uniform(jax.random.fold_in(jax.random.fold_in(rng, 6), axis_at), (blocks,), jnp.float32, low / len(shards), largest / len(shards))
        loudness = loudness * jnp.repeat(jnp.exp(draws), dims[axis_at] // blocks).reshape((-1,) + (1,) * (len(dims) - 1 - axis_at))
    return loudness


def centred(key, shape, deviation, bound, pieces=(), dtype=jnp.bfloat16):
    array = jax.random.normal(key, shape, jnp.float32) * deviation
    if len(pieces) > 0:
        array = block_scale(key, shape, pieces, -0.22, 0.18) * array
    return jnp.clip(array, min=-bound, max=bound).astype(dtype)


def bell_draw_with(rng, extent, scale, reach, cuts, heavy, dtype=jnp.bfloat16):
    entries = scale * jax.random.normal(rng, extent, jnp.float32)
    if cuts:
        entries = entries * block_scale(rng, extent, cuts, -0.22, 0.18)
    return jnp.clip(raised(entries, jax.random.fold_in(rng, 3), *heavy), -reach, reach).astype(dtype)


def setup_inputs(seed: int = 0) -> dict:
    key_list = jax.random.split(jax.random.key(seed), 6)
    wq_flat = bell_draw_with(key_list[0], (D, QW), D ** -0.5, 0.125, ((0, 32),), (0, 1, 32, 2.75))
    hidden = centred(key_list[1], (STEPS, SEQS, D), 1.0, 6.0, ((1, 8),))
    cache = draw_cache(jax.random.fold_in(key_list[5], 71), 0)
    new_kv = centred(key_list[3], (STEPS, SEQS, KVH, 2 * HD), 1.0, 6.0, ((1, 8),))
    lengths = draw_lengths(jax.random.fold_in(key_list[5], 71), 0)
    return dict(wq_flat=wq_flat, hidden=hidden, cache=cache, new_kv=new_kv, lengths=lengths)


def reference(wq_flat, hidden, cache, new_kv, lengths):
    group = QH // KVH
    scale = 1.0 / (HD ** 0.5)
    rows = STEPS * SEQS
    query = jnp.dot(hidden.reshape(rows, D), wq_flat, preferred_element_type=jnp.float32).astype(jnp.bfloat16)
    query = query.reshape(STEPS, SEQS, KVH, group, HD).transpose(1, 0, 2, 3, 4)
    fresh_all = new_kv.transpose(1, 0, 2, 3)
    causal = jnp.arange(STEPS)[:, None] >= jnp.arange(STEPS)[None, :]

    def one_sequence(items):
        queries, stored, fresh, length = items
        queries = queries.astype(jnp.float32)
        keys = stored[..., :HD].astype(jnp.float32)
        values = stored[..., HD:].astype(jnp.float32)
        new_keys = fresh[..., :HD].astype(jnp.float32)
        new_values = fresh[..., HD:].astype(jnp.float32)
        valid = (jnp.arange(CTX) < length)[None, None, None, :]
        old_scores = jnp.einsum("tgjd,gcd->gtjc", queries, keys) * scale
        old_scores = jnp.where(valid, old_scores, -1e30)
        new_scores = jnp.einsum("tgjd,ugd->gtju", queries, new_keys) * scale
        mask_new = causal[None, :, None, :]
        new_scores = jnp.where(mask_new, new_scores, -1e30)
        top = jnp.maximum(jnp.max(old_scores, axis=-1), jnp.max(new_scores, axis=-1))
        old_w = jnp.where(valid, jnp.exp(old_scores - top[..., None]), 0.0)
        new_w = jnp.where(mask_new, jnp.exp(new_scores - top[..., None]), 0.0)
        total = jnp.sum(old_w, axis=-1) + jnp.sum(new_w, axis=-1)
        old_r = old_w.astype(jnp.bfloat16).astype(jnp.float32)
        new_r = new_w.astype(jnp.bfloat16).astype(jnp.float32)
        accum = jnp.einsum("gtjc,gcd->gtjd", old_r, values) + jnp.einsum("gtju,ugd->gtjd", new_r, new_values)
        out = accum / total[..., None]
        return out.transpose(1, 0, 2, 3).reshape(STEPS, QH * HD).astype(jnp.bfloat16)

    result = lax.map(one_sequence, (query, cache, fresh_all, lengths))
    return result.transpose(1, 0, 2)
```

```python
import functools

import jax
import jax.numpy as jnp
from jax import lax
from jax.experimental import pallas as pl
from jax.experimental.pallas import tpu as pltpu
from jax.sharding import PartitionSpec as P

QH = 32
HD = 128
MESH = pl.DeviceIdType.MESH
NEG = -1e30


def kernel(
    n,
    nt,
    lengths,
    hid,
    fresh,
    wq,
    cache,
    out,
    wq_own,
    wq_other,
    kv,
    xg,
    yown,
    ysend,
    yrecv,
    psend,
    precv,
    zsend,
    zrecv,
    qsend,
    qbuf,
    q_sc,
    acc_sc,
    asend,
    arecv,
    m_sc,
    l_sc,
    ssend,
    srecv,
    sem_w,
    sem_kv,
    sx_s,
    sx_r,
    sy_s,
    sy_r,
    sp_s,
    sp_r,
    sz_s,
    sz_r,
    sq_s,
    sq_r,
    sa_s,
    sa_r,
    ss_s,
    ss_r,
):
    d = lax.axis_index("dp")
    t = lax.axis_index("tensor")
    core = lax.rem(d, 2)
    chip = d // 2
    chips = n // 2
    mate = d + 1 - 2 * core
    rows = hid.shape[1]
    half = wq_own.shape[1]
    seqs, kvh, ctx, _ = kv.shape
    heads = QH // nt
    group = QH // kvh
    scale = 1.0 / HD**0.5

    load_other = pltpu.make_async_copy(
        wq.at[:, pl.ds(pl.multiple_of((1 - core) * half, half), half)], wq_other, sem_w.at[0]
    )
    load_own = pltpu.make_async_copy(
        wq.at[:, pl.ds(pl.multiple_of(core * half, half), half)], wq_own, sem_w.at[1]
    )
    load_other.start()
    load_own.start()
    load_kv = [
        [pltpu.make_async_copy(cache.at[s, g], kv.at[s, g], sem_kv.at[s, g]) for g in range(kvh)]
        for s in range(seqs)
    ]
    for g in range(kvh):
        for s in range(seqs):
            load_kv[s][g].start()

    barrier = pltpu.get_barrier_semaphore()

    @pl.loop(1, n)
    def _(k):
        pl.semaphore_signal(
            barrier, inc=1, device_id=(lax.rem(d + k, n), t), device_id_type=MESH
        )

    @pl.loop(1, nt)
    def _(k):
        peer = lax.rem(t + k, nt)
        pl.semaphore_signal(barrier, inc=1, device_id=(d, peer), device_id_type=MESH)
        pl.semaphore_signal(barrier, inc=1, device_id=(mate, peer), device_id_type=MESH)

    pl.semaphore_wait(barrier, n - 1 + 2 * (nt - 1))

    def x_copy(k, slot, peer, source):
        return pltpu.make_async_remote_copy(
            src_ref=hid.at[peer],
            dst_ref=xg.at[slot],
            send_sem=sx_s.at[k],
            recv_sem=sx_r.at[source],
            device_id=(peer, t),
            device_id_type=MESH,
        )

    @pl.loop(1, n)
    def _(k):
        x_copy(k, d, lax.rem(d + k, n), d).start()

    xg[d] = hid[d]
    load_other.wait()
    load_own.wait()

    @pl.loop(1, n)
    def _(k):
        peer = lax.rem(d + k, n)
        x_copy(k, peer, peer, peer).wait_recv()

    x = xg[...].reshape(n * rows, xg.shape[2]).astype(jnp.bfloat16)

    psend[...] = (
        jnp.dot(x, wq_other[...], preferred_element_type=jnp.float32)
        .astype(jnp.bfloat16)
        .reshape(chips, 2 * rows, half)
    )

    def p_copy(p):
        return pltpu.make_async_remote_copy(
            src_ref=psend.at[p],
            dst_ref=precv.at[p],
            send_sem=sp_s.at[p],
            recv_sem=sp_r.at[p],
            device_id=(mate, t),
            device_id_type=MESH,
        )

    def order(k):
        return lax.rem(chip + chips - k, chips)

    @pl.loop(1, chips + 1)
    def _(k):
        p_copy(order(k)).start()

    yown[...] = jnp.dot(x, wq_own[...], preferred_element_type=jnp.float32).reshape(
        chips, 2 * rows, half
    )

    def y_copy(k, slot, peer, source):
        return pltpu.make_async_remote_copy(
            src_ref=ysend.at[peer],
            dst_ref=yrecv.at[slot],
            send_sem=sy_s.at[k],
            recv_sem=sy_r.at[source],
            device_id=(2 * peer + core, t),
            device_id_type=MESH,
        )

    @pl.loop(1, chips)
    def _(k):
        p = order(k)
        p_copy(p).wait_recv()
        ysend[p] = (yown[p] + precv[p].astype(jnp.float32)).astype(jnp.bfloat16)
        y_copy(k, chip, p, chip).start()

    p_copy(chip).wait_recv()
    z0 = yown[chip] + precv[chip].astype(jnp.float32)

    def y_add(k, z):
        p = order(k)
        y_copy(k, p, p, p).wait_recv()
        return z + yrecv[p].astype(jnp.float32)

    z = lax.fori_loop(1, chips, y_add, z0)

    part = half // nt
    for j in range(nt):
        zsend[j] = z[:, j * part : (j + 1) * part].astype(zsend.dtype)

    def z_copy(k, slot, peer, source):
        return pltpu.make_async_remote_copy(
            src_ref=zsend.at[peer],
            dst_ref=zrecv.at[slot],
            send_sem=sz_s.at[k],
            recv_sem=sz_r.at[source],
            device_id=(d, peer),
            device_id_type=MESH,
        )

    @pl.loop(1, nt)
    def _(k):
        z_copy(k, t, lax.rem(t + k, nt), t).start()

    def z_add(k, total):
        peer = lax.rem(t + k, nt)
        z_copy(k, peer, peer, peer).wait_recv()
        return total + zrecv[peer].astype(jnp.float32)

    piece = lax.fori_loop(1, nt, z_add, zsend[t].astype(jnp.float32))
    for c in range(2):
        qsend[c] = piece[c * rows : (c + 1) * rows].astype(jnp.bfloat16)

    def q_copy(k, which, peer_core, peer, slot):
        return pltpu.make_async_remote_copy(
            src_ref=qsend.at[peer_core],
            dst_ref=qbuf.at[slot],
            send_sem=sq_s.at[k, which],
            recv_sem=sq_r.at[slot],
            device_id=(2 * chip + peer_core, peer),
            device_id_type=MESH,
        )

    mine = core * nt + t

    @pl.loop(1, nt)
    def _(k):
        peer = lax.rem(t + k, nt)
        q_copy(k, 0, core, peer, mine).start()
        q_copy(k, 1, 1 - core, peer, mine).start()

    q_copy(0, 1, 1 - core, t, mine).start()
    qbuf[mine] = qsend[core]
    q_copy(0, 1, 1 - core, t, (1 - core) * nt + t).wait_recv()

    @pl.loop(1, nt)
    def _(k):
        peer = lax.rem(t + k, nt)
        q_copy(k, 0, core, peer, core * nt + peer).wait_recv()
        q_copy(k, 1, core, peer, (1 - core) * nt + peer).wait_recv()

    heads_slot = part // HD
    for slot in range(2 * nt):
        block = qbuf[slot].astype(jnp.float32)
        for j in range(heads_slot):
            h = slot * heads_slot + j
            q_sc[h * rows : (h + 1) * rows, :] = block[:, j * HD : (j + 1) * HD]

    steps = rows // seqs
    band = group * rows
    position = t * ctx + lax.broadcasted_iota(jnp.int32, (1, ctx), 1)
    owned = heads * rows

    def a_copy(k, slot, peer, source):
        return pltpu.make_async_remote_copy(
            src_ref=asend.at[peer],
            dst_ref=arecv.at[slot],
            send_sem=sa_s.at[k],
            recv_sem=sa_r.at[source],
            device_id=(d, peer),
            device_id_type=MESH,
        )

    def s_copy(k, slot, peer, source):
        return pltpu.make_async_remote_copy(
            src_ref=ssend.at[peer],
            dst_ref=srecv.at[slot],
            send_sem=ss_s.at[k],
            recv_sem=ss_r.at[source],
            device_id=(d, peer),
            device_id_type=MESH,
        )

    for g in range(kvh):
        for s in range(seqs):
            load_kv[s][g].wait()
            span = pl.ds(g * band + s, group * steps, stride=seqs)
            q = q_sc[span, :].astype(jnp.bfloat16)
            scores = (
                lax.dot_general(
                    q,
                    kv[s, g, :, :HD],
                    (((1,), (1,)), ((), ())),
                    preferred_element_type=jnp.float32,
                )
                * scale
            )
            valid = position < lengths[s]
            masked = jnp.where(valid, scores, NEG)
            best = jnp.max(masked, axis=-1, keepdims=True)
            weights = jnp.where(valid, jnp.exp(masked - best), 0.0)
            total = jnp.sum(weights, axis=-1, keepdims=True)
            acc = jnp.dot(
                weights.astype(jnp.bfloat16), kv[s, g, :, HD:], preferred_element_type=jnp.float32
            )
            acc_sc[span, :] = acc
            m_sc[span, :] = jnp.broadcast_to(best, acc.shape)
            l_sc[span, :] = jnp.broadcast_to(total, acc.shape)

    eye = lax.broadcasted_iota(jnp.int32, (owned, HD), 0) == lax.broadcasted_iota(
        jnp.int32, (owned, HD), 1
    )
    for j in range(nt):
        window = slice(j * owned, (j + 1) * owned)
        asend[j] = acc_sc[window, :].astype(asend.dtype)
        ssend[j, 0:1, :] = jnp.sum(jnp.where(eye, m_sc[window, :], 0.0), axis=0, keepdims=True)
        ssend[j, 1:2, :] = jnp.sum(jnp.where(eye, l_sc[window, :], 0.0), axis=0, keepdims=True)

    @pl.loop(1, nt)
    def _(k):
        peer = lax.rem(t + k, nt)
        a_copy(k, t, peer, t).start()
        s_copy(k, t, peer, t).start()

    own = pl.ds(pl.multiple_of(t * owned, owned), owned)
    q_own = q_sc[own, :].astype(jnp.bfloat16)
    new_scores = (
        lax.dot_general(
            q_own, fresh[:, :HD], (((1,), (1,)), ((), ())), preferred_element_type=jnp.float32
        )
        * scale
    )
    row = lax.broadcasted_iota(jnp.int32, new_scores.shape, 0)
    col = lax.broadcasted_iota(jnp.int32, new_scores.shape, 1)
    row_seq = lax.rem(row, seqs)
    row_step = lax.rem(row, rows) // seqs
    causal = (row_seq == lax.rem(col, seqs)) & (row_step >= col // seqs)
    new_masked = jnp.where(causal, new_scores, NEG)
    top = jnp.max(new_masked, axis=-1, keepdims=True)
    new_weights = jnp.where(causal, jnp.exp(new_masked - top), 0.0)
    denom = jnp.sum(new_weights, axis=-1, keepdims=True)
    accum = jnp.dot(
        new_weights.astype(jnp.bfloat16), fresh[:, HD:], preferred_element_type=jnp.float32
    )

    def join(state, best, total, acc):
        top, denom, accum = state
        peak = jnp.maximum(top, best)
        left = jnp.exp(top - peak)
        right = jnp.exp(best - peak)
        return peak, denom * left + total * right, accum * left + acc * right

    state = join((top, denom, accum), m_sc[own, :][:, :1], l_sc[own, :][:, :1], acc_sc[own, :])

    def a_join(k, state):
        peer = lax.rem(t + k, nt)
        a_copy(k, peer, peer, peer).wait_recv()
        s_copy(k, peer, peer, peer).wait_recv()
        stats = srecv[peer]
        best = jnp.sum(jnp.where(eye, stats[0:1, :], 0.0), axis=1, keepdims=True)
        total = jnp.sum(jnp.where(eye, stats[1:2, :], 0.0), axis=1, keepdims=True)
        return join(state, best, total, arecv[peer].astype(jnp.float32))

    top, denom, accum = lax.fori_loop(1, nt, a_join, state)
    result = accum / denom
    for j in range(heads):
        out[:, j * HD : (j + 1) * HD] = result[j * rows : (j + 1) * rows].astype(out.dtype)

    @pl.loop(1, n)
    def _(k):
        x_copy(k, d, lax.rem(d + k, n), d).wait_send()

    @pl.loop(1, chips + 1)
    def _(k):
        p_copy(order(k)).wait_send()

    @pl.loop(1, chips)
    def _(k):
        y_copy(k, chip, order(k), chip).wait_send()

    q_copy(0, 1, 1 - core, t, mine).wait_send()

    @pl.loop(1, nt)
    def _(k):
        peer = lax.rem(t + k, nt)
        z_copy(k, t, peer, t).wait_send()
        q_copy(k, 0, core, peer, mine).wait_send()
        q_copy(k, 1, 1 - core, peer, mine).wait_send()
        a_copy(k, t, peer, t).wait_send()
        s_copy(k, t, peer, t).wait_send()


def body(wq_flat, hidden, cache, new_kv, lengths):
    nt = lax.axis_size("tensor")
    n = lax.axis_size("dp")
    t = lax.axis_index("tensor")
    steps, seqs, width = hidden.shape
    rows = steps * seqs
    depth, columns = wq_flat.shape
    kvh, ctx = cache.shape[1], cache.shape[2]
    half = columns // 2
    part = half // nt
    heads = QH // nt
    group = QH // kvh
    owned = heads * rows
    chips = n // 2
    blocks = hidden.reshape(rows, n, nt, depth)
    hid = lax.dynamic_index_in_dim(blocks, t, 2, keepdims=False).astype(jnp.float32)
    hid = hid.transpose(1, 0, 2)
    fresh = lax.dynamic_index_in_dim(new_kv, t * heads // group, 2, keepdims=False)
    fresh = jnp.pad(fresh.reshape(rows, 2 * HD), ((0, HD - rows), (0, 0)))
    bf16, f32 = jnp.bfloat16, jnp.float32
    dma = pltpu.SemaphoreType.DMA
    vmem = pl.BlockSpec(memory_space=pltpu.VMEM)
    anywhere = pl.BlockSpec(memory_space=pl.ANY)
    result = pl.pallas_call(
        functools.partial(kernel, n, nt),
        out_shape=jax.ShapeDtypeStruct((rows, heads * HD), bf16),
        in_specs=[pl.BlockSpec(memory_space=pltpu.SMEM), vmem, vmem, anywhere, anywhere],
        out_specs=vmem,
        scratch_shapes=[
            pltpu.VMEM((depth, half), bf16),
            pltpu.VMEM((depth, half), bf16),
            pltpu.VMEM(cache.shape, bf16),
            pltpu.VMEM((n, rows, depth), f32),
            pltpu.VMEM((chips, 2 * rows, half), f32),
            pltpu.VMEM((chips, 2 * rows, half), bf16),
            pltpu.VMEM((chips, 2 * rows, half), bf16),
            pltpu.VMEM((chips, 2 * rows, half), bf16),
            pltpu.VMEM((chips, 2 * rows, half), bf16),
            pltpu.VMEM((nt, 2 * rows, part), bf16),
            pltpu.VMEM((nt, 2 * rows, part), bf16),
            pltpu.VMEM((2, rows, part), bf16),
            pltpu.VMEM((2 * nt, rows, part), bf16),
            pltpu.VMEM((QH * rows, HD), f32),
            pltpu.VMEM((QH * rows, HD), f32),
            pltpu.VMEM((nt, owned, HD), bf16),
            pltpu.VMEM((nt, owned, HD), bf16),
            pltpu.VMEM((QH * rows, HD), f32),
            pltpu.VMEM((QH * rows, HD), f32),
            pltpu.VMEM((nt, 8, HD), f32),
            pltpu.VMEM((nt, 8, HD), f32),
            dma((2,)),
            dma((seqs, kvh)),
            dma((n,)),
            dma((n,)),
            dma((chips,)),
            dma((chips,)),
            dma((chips,)),
            dma((chips,)),
            dma((nt,)),
            dma((nt,)),
            dma((nt, 2)),
            dma((2 * nt,)),
            dma((nt,)),
            dma((nt,)),
            dma((nt,)),
            dma((nt,)),
        ],
        compiler_params=pltpu.CompilerParams(collective_id=0, has_side_effects=True),
    )(lengths, hid, fresh, wq_flat, cache)
    return result.reshape(steps, seqs, heads * HD)


def solution(mesh):
    placed = (
        P(("dp", "tensor"), None),
        P(None, "dp", None),
        P("dp", None, "tensor", None),
        P(None, "dp", None, None),
        P("dp"),
    )
    return jax.shard_map(
        body, mesh=mesh, in_specs=placed, out_specs=P(None, "dp", "tensor"), check_vma=False
    )
```

```python
import functools

import jax
import jax.numpy as jnp
from jax import lax
from jax.experimental import pallas as pl
from jax.experimental.pallas import tpu as pltpu
from jax.sharding import PartitionSpec as P

QH = 32
HD = 128
MESH = pl.DeviceIdType.MESH
NEG = -1e30


def kernel(
    n,
    nt,
    blocked,
    lengths,
    hid,
    blocks,
    new_kv,
    wq,
    cache,
    out,
    wq_own,
    wq_other,
    kv,
    fresh,
    x_sc,
    xg,
    yown,
    ysend,
    yrecv,
    psend,
    precv,
    zsend,
    zrecv,
    qsend,
    qbuf,
    q_sc,
    acc_sc,
    asend,
    arecv,
    m_sc,
    l_sc,
    ssend,
    srecv,
    sem_w,
    sem_kv,
    sx_s,
    sx_r,
    sy_s,
    sy_r,
    sp_s,
    sp_r,
    sz_s,
    sz_r,
    sq_s,
    sq_r,
    sa_s,
    sa_r,
    ss_s,
    ss_r,
):
    d = lax.axis_index("dp")
    t = lax.axis_index("tensor")
    core = lax.rem(d, 2)
    chip = d // 2
    chips = n // 2
    mate = d + 1 - 2 * core
    steps, seqs, width = hid.shape
    depth = wq_own.shape[0]
    rows = steps * seqs
    half = wq_own.shape[1]
    _, kvh, ctx, _ = kv.shape
    drains = []
    heads = QH // nt
    group = QH // kvh
    scale = 1.0 / HD**0.5

    load_other = pltpu.make_async_copy(
        wq.at[:, pl.ds(pl.multiple_of((1 - core) * half, half), half)], wq_other, sem_w.at[0]
    )
    load_own = pltpu.make_async_copy(
        wq.at[:, pl.ds(pl.multiple_of(core * half, half), half)], wq_own, sem_w.at[1]
    )
    load_other.start()
    load_own.start()
    load_kv = [
        [pltpu.make_async_copy(cache.at[s, g], kv.at[s, g], sem_kv.at[s, g]) for g in range(kvh)]
        for s in range(seqs)
    ]
    for g in range(kvh):
        for s in range(seqs):
            load_kv[s][g].start()

    barrier = pltpu.get_barrier_semaphore()

    @pl.loop(1, n)
    def _(k):
        pl.semaphore_signal(
            barrier, inc=1, device_id=(lax.rem(d + k, n), t), device_id_type=MESH
        )

    @pl.loop(1, nt)
    def _(k):
        peer = lax.rem(t + k, nt)
        pl.semaphore_signal(barrier, inc=1, device_id=(d, peer), device_id_type=MESH)
        pl.semaphore_signal(barrier, inc=1, device_id=(mate, peer), device_id_type=MESH)

    pl.semaphore_wait(barrier, n - 1 + 2 * (nt - 1))

    def columns_of(peer):
        if blocked:
            return blocks.at[peer]
        start = pl.multiple_of((peer * nt + t) * depth, depth)
        return hid.at[:, :, pl.ds(start, depth)]

    def x_copy(k, slot, peer, source):
        return pltpu.make_async_remote_copy(
            src_ref=columns_of(peer),
            dst_ref=xg.at[slot],
            send_sem=sx_s.at[k],
            recv_sem=sx_r.at[source],
            device_id=(peer, t),
            device_id_type=MESH,
        )

    @pl.loop(1, n)
    def _(k):
        x_copy(k, d, lax.rem(d + k, n), d).start()

    xg[d] = columns_of(d)[...]
    for i in range(steps):
        for s in range(seqs):
            r = (i * seqs + s) * kvh
            fresh[r : r + kvh, :] = new_kv[i, s].astype(jnp.float32)
    load_other.wait()
    load_own.wait()

    @pl.loop(1, n)
    def _(k):
        peer = lax.rem(d + k, n)
        x_copy(k, peer, peer, peer).wait_recv()

    drains.append(lambda: pl.loop(1, n)(lambda k: x_copy(k, d, lax.rem(d + k, n), d).wait_send()))
    if blocked:
        x = xg[...].reshape(n * rows, depth).astype(jnp.bfloat16)
    else:
        for p in range(n):
            for i in range(steps):
                r = p * rows + i * seqs
                x_sc[r : r + seqs, :] = xg[p, i].astype(jnp.float32)
        x = x_sc[...].astype(jnp.bfloat16)

    psend[...] = (
        jnp.dot(x, wq_other[...], preferred_element_type=jnp.float32)
        .astype(jnp.bfloat16)
        .reshape(chips, 2 * rows, half)
    )

    def p_copy(p):
        return pltpu.make_async_remote_copy(
            src_ref=psend.at[p],
            dst_ref=precv.at[p],
            send_sem=sp_s.at[p],
            recv_sem=sp_r.at[p],
            device_id=(mate, t),
            device_id_type=MESH,
        )

    def order(k):
        return lax.rem(chip + chips - k, chips)

    @pl.loop(1, chips + 1)
    def _(k):
        p_copy(order(k)).start()

    yown[...] = jnp.dot(x, wq_own[...], preferred_element_type=jnp.float32).reshape(
        chips, 2 * rows, half
    )

    drains.append(lambda: pl.loop(1, chips + 1)(lambda k: p_copy(order(k)).wait_send()))

    def y_copy(k, slot, peer, source):
        return pltpu.make_async_remote_copy(
            src_ref=ysend.at[peer],
            dst_ref=yrecv.at[slot],
            send_sem=sy_s.at[k],
            recv_sem=sy_r.at[source],
            device_id=(2 * peer + core, t),
            device_id_type=MESH,
        )

    @pl.loop(1, chips)
    def _(k):
        p = order(k)
        p_copy(p).wait_recv()
        ysend[p] = (yown[p] + precv[p].astype(jnp.float32)).astype(jnp.bfloat16)
        y_copy(k, chip, p, chip).start()

    p_copy(chip).wait_recv()
    z0 = yown[chip] + precv[chip].astype(jnp.float32)

    def y_add(k, z):
        p = order(k)
        y_copy(k, p, p, p).wait_recv()
        return z + yrecv[p].astype(jnp.float32)

    z = lax.fori_loop(1, chips, y_add, z0)

    drains.append(lambda: pl.loop(1, chips)(lambda k: y_copy(k, chip, order(k), chip).wait_send()))

    part = half // nt
    for j in range(nt):
        zsend[j] = z[:, j * part : (j + 1) * part].astype(zsend.dtype)

    def z_copy(k, slot, peer, source):
        return pltpu.make_async_remote_copy(
            src_ref=zsend.at[peer],
            dst_ref=zrecv.at[slot],
            send_sem=sz_s.at[k],
            recv_sem=sz_r.at[source],
            device_id=(d, peer),
            device_id_type=MESH,
        )

    @pl.loop(1, nt)
    def _(k):
        z_copy(k, t, lax.rem(t + k, nt), t).start()

    def z_add(k, total):
        peer = lax.rem(t + k, nt)
        z_copy(k, peer, peer, peer).wait_recv()
        return total + zrecv[peer].astype(jnp.float32)

    piece = lax.fori_loop(1, nt, z_add, zsend[t].astype(jnp.float32))
    for c in range(2):
        qsend[c] = piece[c * rows : (c + 1) * rows].astype(jnp.bfloat16)

    drains.append(
        lambda: pl.loop(1, nt)(lambda k: z_copy(k, t, lax.rem(t + k, nt), t).wait_send())
    )

    def q_copy(k, which, peer_core, peer, slot):
        return pltpu.make_async_remote_copy(
            src_ref=qsend.at[peer_core],
            dst_ref=qbuf.at[slot],
            send_sem=sq_s.at[k, which],
            recv_sem=sq_r.at[slot],
            device_id=(2 * chip + peer_core, peer),
            device_id_type=MESH,
        )

    mine = core * nt + t

    @pl.loop(1, nt)
    def _(k):
        peer = lax.rem(t + k, nt)
        q_copy(k, 0, core, peer, mine).start()
        q_copy(k, 1, 1 - core, peer, mine).start()

    q_copy(0, 1, 1 - core, t, mine).start()
    qbuf[mine] = qsend[core]
    q_copy(0, 1, 1 - core, t, (1 - core) * nt + t).wait_recv()

    @pl.loop(1, nt)
    def _(k):
        peer = lax.rem(t + k, nt)
        q_copy(k, 0, core, peer, core * nt + peer).wait_recv()
        q_copy(k, 1, core, peer, (1 - core) * nt + peer).wait_recv()

    def q_drain():
        q_copy(0, 1, 1 - core, t, mine).wait_send()

        @pl.loop(1, nt)
        def _(k):
            peer = lax.rem(t + k, nt)
            q_copy(k, 0, core, peer, mine).wait_send()
            q_copy(k, 1, 1 - core, peer, mine).wait_send()

    drains.append(q_drain)
    heads_slot = part // HD
    for slot in range(2 * nt):
        block = qbuf[slot].astype(jnp.float32)
        for j in range(heads_slot):
            h = slot * heads_slot + j
            q_sc[h * rows : (h + 1) * rows, :] = block[:, j * HD : (j + 1) * HD]

    band = group * rows
    position = t * ctx + lax.broadcasted_iota(jnp.int32, (1, ctx), 1)
    owned = heads * rows

    def a_copy(k, slot, peer, source):
        return pltpu.make_async_remote_copy(
            src_ref=asend.at[peer],
            dst_ref=arecv.at[slot],
            send_sem=sa_s.at[k],
            recv_sem=sa_r.at[source],
            device_id=(d, peer),
            device_id_type=MESH,
        )

    def s_copy(k, slot, peer, source):
        return pltpu.make_async_remote_copy(
            src_ref=ssend.at[peer],
            dst_ref=srecv.at[slot],
            send_sem=ss_s.at[k],
            recv_sem=ss_r.at[source],
            device_id=(d, peer),
            device_id_type=MESH,
        )

    for g in range(kvh):
        for s in range(seqs):
            load_kv[s][g].wait()
            span = pl.ds(g * band + s, group * steps, stride=seqs)
            q = q_sc[span, :].astype(jnp.bfloat16)
            scores = (
                lax.dot_general(
                    q,
                    kv[s, g, :, :HD],
                    (((1,), (1,)), ((), ())),
                    preferred_element_type=jnp.float32,
                )
                * scale
            )
            valid = position < lengths[s]
            masked = jnp.where(valid, scores, NEG)
            best = jnp.max(masked, axis=-1, keepdims=True)
            weights = jnp.where(valid, jnp.exp(masked - best), 0.0)
            total = jnp.sum(weights, axis=-1, keepdims=True)
            acc = jnp.dot(
                weights.astype(jnp.bfloat16), kv[s, g, :, HD:], preferred_element_type=jnp.float32
            )
            acc_sc[span, :] = acc
            m_sc[span, :] = jnp.broadcast_to(best, acc.shape)
            l_sc[span, :] = jnp.broadcast_to(total, acc.shape)

    eye = lax.broadcasted_iota(jnp.int32, (owned, HD), 0) == lax.broadcasted_iota(
        jnp.int32, (owned, HD), 1
    )
    for j in range(nt):
        window = slice(j * owned, (j + 1) * owned)
        asend[j] = acc_sc[window, :].astype(asend.dtype)
        ssend[j, 0:1, :] = jnp.sum(jnp.where(eye, m_sc[window, :], 0.0), axis=0, keepdims=True)
        ssend[j, 1:2, :] = jnp.sum(jnp.where(eye, l_sc[window, :], 0.0), axis=0, keepdims=True)

    @pl.loop(1, nt)
    def _(k):
        peer = lax.rem(t + k, nt)
        a_copy(k, t, peer, t).start()
        s_copy(k, t, peer, t).start()

    own = pl.ds(pl.multiple_of(t * owned, owned), owned)
    q_own = q_sc[own, :].astype(jnp.bfloat16)
    new_keys = fresh[:, :HD].astype(jnp.bfloat16)
    new_values = fresh[:, HD:].astype(jnp.bfloat16)
    new_scores = (
        lax.dot_general(
            q_own, new_keys, (((1,), (1,)), ((), ())), preferred_element_type=jnp.float32
        )
        * scale
    )
    row = lax.broadcasted_iota(jnp.int32, new_scores.shape, 0)
    col = lax.broadcasted_iota(jnp.int32, new_scores.shape, 1)
    col_row = col // kvh
    causal = (
        (lax.rem(col, kvh) == t * heads // group)
        & (lax.rem(row, seqs) == lax.rem(col_row, seqs))
        & (lax.rem(row, rows) // seqs >= col_row // seqs)
    )
    new_masked = jnp.where(causal, new_scores, NEG)
    top = jnp.max(new_masked, axis=-1, keepdims=True)
    new_weights = jnp.where(causal, jnp.exp(new_masked - top), 0.0)
    denom = jnp.sum(new_weights, axis=-1, keepdims=True)
    accum = jnp.dot(
        new_weights.astype(jnp.bfloat16), new_values, preferred_element_type=jnp.float32
    )

    def join(state, best, total, acc):
        top, denom, accum = state
        peak = jnp.maximum(top, best)
        left = jnp.exp(top - peak)
        right = jnp.exp(best - peak)
        return peak, denom * left + total * right, accum * left + acc * right

    state = join((top, denom, accum), m_sc[own, :][:, :1], l_sc[own, :][:, :1], acc_sc[own, :])

    def a_join(k, state):
        peer = lax.rem(t + k, nt)
        a_copy(k, peer, peer, peer).wait_recv()
        s_copy(k, peer, peer, peer).wait_recv()
        stats = srecv[peer]
        best = jnp.sum(jnp.where(eye, stats[0:1, :], 0.0), axis=1, keepdims=True)
        total = jnp.sum(jnp.where(eye, stats[1:2, :], 0.0), axis=1, keepdims=True)
        return join(state, best, total, arecv[peer].astype(jnp.float32))

    top, denom, accum = lax.fori_loop(1, nt, a_join, state)
    result = accum / denom
    for j in range(heads):
        for i in range(steps):
            r = j * rows + i * seqs
            out[i, :, j * HD : (j + 1) * HD] = result[r : r + seqs].astype(out.dtype)

    def a_drain():
        @pl.loop(1, nt)
        def _(k):
            peer = lax.rem(t + k, nt)
            a_copy(k, t, peer, t).wait_send()
            s_copy(k, t, peer, t).wait_send()

    drains.append(a_drain)
    for drain in drains:
        drain()


def body(wq_flat, hidden, cache, new_kv, lengths):
    nt = lax.axis_size("tensor")
    n = lax.axis_size("dp")
    t = lax.axis_index("tensor")
    steps, seqs, width = hidden.shape
    rows = steps * seqs
    depth, columns = wq_flat.shape
    kvh, ctx = cache.shape[1], cache.shape[2]
    half = columns // 2
    part = half // nt
    heads = QH // nt
    owned = heads * rows
    chips = n // 2
    bf16, f32 = jnp.bfloat16, jnp.float32
    dma = pltpu.SemaphoreType.DMA
    vmem = pl.BlockSpec(memory_space=pltpu.VMEM)
    blocked = depth % 128 != 0
    blocks = hidden
    if blocked:
        blocks = hidden.reshape(rows, n, nt, depth)
        blocks = lax.dynamic_index_in_dim(blocks, t, 2, keepdims=False).astype(f32)
        blocks = blocks.transpose(1, 0, 2)
    held = (rows, depth) if blocked else (steps, seqs, depth)
    anywhere = pl.BlockSpec(memory_space=pl.ANY)
    return pl.pallas_call(
        functools.partial(kernel, n, nt, blocked),
        out_shape=jax.ShapeDtypeStruct((steps, seqs, heads * HD), bf16),
        in_specs=[pl.BlockSpec(memory_space=pltpu.SMEM), vmem, vmem, vmem, anywhere, anywhere],
        out_specs=vmem,
        scratch_shapes=[
            pltpu.VMEM((depth, half), bf16),
            pltpu.VMEM((depth, half), bf16),
            pltpu.VMEM(cache.shape, bf16),
            pltpu.VMEM((rows * kvh, 2 * HD), f32),
            pltpu.VMEM((n * rows, depth), f32),
            pltpu.VMEM((n, *held), blocks.dtype),
            pltpu.VMEM((chips, 2 * rows, half), f32),
            pltpu.VMEM((chips, 2 * rows, half), bf16),
            pltpu.VMEM((chips, 2 * rows, half), bf16),
            pltpu.VMEM((chips, 2 * rows, half), bf16),
            pltpu.VMEM((chips, 2 * rows, half), bf16),
            pltpu.VMEM((nt, 2 * rows, part), bf16),
            pltpu.VMEM((nt, 2 * rows, part), bf16),
            pltpu.VMEM((2, rows, part), bf16),
            pltpu.VMEM((2 * nt, rows, part), bf16),
            pltpu.VMEM((QH * rows, HD), f32),
            pltpu.VMEM((QH * rows, HD), f32),
            pltpu.VMEM((nt, owned, HD), bf16),
            pltpu.VMEM((nt, owned, HD), bf16),
            pltpu.VMEM((QH * rows, HD), f32),
            pltpu.VMEM((QH * rows, HD), f32),
            pltpu.VMEM((nt, 8, HD), f32),
            pltpu.VMEM((nt, 8, HD), f32),
            dma((2,)),
            dma((seqs, kvh)),
            dma((n,)),
            dma((n,)),
            dma((chips,)),
            dma((chips,)),
            dma((chips,)),
            dma((chips,)),
            dma((nt,)),
            dma((nt,)),
            dma((nt, 2)),
            dma((2 * nt,)),
            dma((nt,)),
            dma((nt,)),
            dma((nt,)),
            dma((nt,)),
        ],
        compiler_params=pltpu.CompilerParams(collective_id=0, has_side_effects=True),
    )(lengths, hidden, blocks, new_kv, wq_flat, cache)


def solution(mesh):
    placed = (
        P(("dp", "tensor"), None),
        P(None, "dp", None),
        P("dp", None, "tensor", None),
        P(None, "dp", None, None),
        P("dp"),
    )
    return jax.shard_map(
        body, mesh=mesh, in_specs=placed, out_specs=P(None, "dp", "tensor"), check_vma=False
    )
```

```python
import functools

import jax
import jax.numpy as jnp
from jax import lax
from jax.experimental import pallas as pl
from jax.experimental.pallas import tpu as pltpu
from jax.sharding import PartitionSpec as P

QH = 32
HD = 128
MESH = pl.DeviceIdType.MESH
NEG = -1e30


def kernel(
    n,
    nt,
    blocked,
    lengths,
    hid_any,
    blocks,
    new_any,
    wq,
    cache,
    out,
    hid,
    new_kv,
    sem_in,
    wq_own,
    wq_other,
    kv,
    fresh,
    x_sc,
    xg,
    yown,
    ysend,
    yrecv,
    psend,
    precv,
    zsend,
    zrecv,
    qsend,
    qbuf,
    q_sc,
    acc_sc,
    asend,
    arecv,
    m_sc,
    l_sc,
    ssend,
    srecv,
    sem_w,
    sem_kv,
    sx_s,
    sx_r,
    sy_s,
    sy_r,
    sp_s,
    sp_r,
    sz_s,
    sz_r,
    sq_s,
    sq_r,
    sa_s,
    sa_r,
    ss_s,
    ss_r,
):
    d = lax.axis_index("dp")
    t = lax.axis_index("tensor")
    core = lax.rem(d, 2)
    chip = d // 2
    chips = n // 2
    mate = d + 1 - 2 * core
    steps, seqs, width = hid.shape
    depth = wq_own.shape[0]
    rows = steps * seqs
    half = wq_own.shape[1]
    _, kvh, ctx, _ = kv.shape
    drains = []
    heads = QH // nt
    group = QH // kvh
    scale = 1.0 / HD**0.5

    load_hid = pltpu.make_async_copy(hid_any, hid, sem_in.at[0])
    load_new = pltpu.make_async_copy(new_any, new_kv, sem_in.at[1])
    load_hid.start()
    load_new.start()
    load_other = pltpu.make_async_copy(
        wq.at[:, pl.ds(pl.multiple_of((1 - core) * half, half), half)], wq_other, sem_w.at[0]
    )
    load_own = pltpu.make_async_copy(
        wq.at[:, pl.ds(pl.multiple_of(core * half, half), half)], wq_own, sem_w.at[1]
    )
    load_other.start()
    load_own.start()
    load_kv = [
        [pltpu.make_async_copy(cache.at[s, g], kv.at[s, g], sem_kv.at[s, g]) for g in range(kvh)]
        for s in range(seqs)
    ]
    for g in range(kvh):
        for s in range(seqs):
            load_kv[s][g].start()

    barrier = pltpu.get_barrier_semaphore()

    @pl.loop(1, n)
    def _(k):
        pl.semaphore_signal(
            barrier, inc=1, device_id=(lax.rem(d + k, n), t), device_id_type=MESH
        )

    @pl.loop(1, nt)
    def _(k):
        peer = lax.rem(t + k, nt)
        pl.semaphore_signal(barrier, inc=1, device_id=(d, peer), device_id_type=MESH)
        pl.semaphore_signal(barrier, inc=1, device_id=(mate, peer), device_id_type=MESH)

    pl.semaphore_wait(barrier, n - 1 + 2 * (nt - 1))

    load_hid.wait()
    load_new.wait()

    def columns_of(peer):
        if blocked:
            return blocks.at[peer]
        start = pl.multiple_of((peer * nt + t) * depth, depth)
        return hid.at[:, :, pl.ds(start, depth)]

    def x_copy(k, slot, peer, source):
        return pltpu.make_async_remote_copy(
            src_ref=columns_of(peer),
            dst_ref=xg.at[slot],
            send_sem=sx_s.at[k],
            recv_sem=sx_r.at[source],
            device_id=(peer, t),
            device_id_type=MESH,
        )

    @pl.loop(1, n)
    def _(k):
        x_copy(k, d, lax.rem(d + k, n), d).start()

    xg[d] = columns_of(d)[...]
    for i in range(steps):
        for s in range(seqs):
            r = (i * seqs + s) * kvh
            fresh[r : r + kvh, :] = new_kv[i, s].astype(jnp.float32)
    load_other.wait()
    load_own.wait()

    @pl.loop(1, n)
    def _(k):
        peer = lax.rem(d + k, n)
        x_copy(k, peer, peer, peer).wait_recv()

    drains.append(lambda: pl.loop(1, n)(lambda k: x_copy(k, d, lax.rem(d + k, n), d).wait_send()))
    if blocked:
        x = xg[...].reshape(n * rows, depth).astype(jnp.bfloat16)
    else:
        for p in range(n):
            for i in range(steps):
                r = p * rows + i * seqs
                x_sc[r : r + seqs, :] = xg[p, i].astype(jnp.float32)
        x = x_sc[...].astype(jnp.bfloat16)

    cuts = psend.shape[0]
    wide = half // cuts

    def p_copy(c, p):
        return pltpu.make_async_remote_copy(
            src_ref=psend.at[c, p],
            dst_ref=precv.at[c, p],
            send_sem=sp_s.at[c, p],
            recv_sem=sp_r.at[c, p],
            device_id=(mate, t),
            device_id_type=MESH,
        )

    def order(k):
        return lax.rem(chip + chips - k, chips)

    for c in range(cuts):
        psend[c] = (
            jnp.dot(
                x, wq_other[:, c * wide : (c + 1) * wide], preferred_element_type=jnp.float32
            )
            .astype(jnp.bfloat16)
            .reshape(chips, 2 * rows, wide)
        )

        @pl.loop(1, chips + 1)
        def _(k):
            p_copy(c, order(k)).start()

    for c in range(cuts):
        yown[c] = jnp.dot(
            x, wq_own[:, c * wide : (c + 1) * wide], preferred_element_type=jnp.float32
        ).reshape(chips, 2 * rows, wide)

    def p_drain():
        for c in range(cuts):
            pl.loop(1, chips + 1)(lambda k: p_copy(c, order(k)).wait_send())

    drains.append(p_drain)

    def y_copy(c, k, slot, peer, source):
        return pltpu.make_async_remote_copy(
            src_ref=ysend.at[c, peer],
            dst_ref=yrecv.at[c, slot],
            send_sem=sy_s.at[c, k],
            recv_sem=sy_r.at[c, source],
            device_id=(2 * peer + core, t),
            device_id_type=MESH,
        )

    for c in range(cuts):

        @pl.loop(1, chips)
        def _(k):
            p = order(k)
            p_copy(c, p).wait_recv()
            ysend[c, p] = (yown[c, p] + precv[c, p].astype(jnp.float32)).astype(jnp.bfloat16)
            y_copy(c, k, chip, p, chip).start()

        p_copy(c, chip).wait_recv()

    part = wide // nt

    def z_copy(c, k, slot, peer, source):
        return pltpu.make_async_remote_copy(
            src_ref=zsend.at[c, peer],
            dst_ref=zrecv.at[c, slot],
            send_sem=sz_s.at[c, k],
            recv_sem=sz_r.at[c, source],
            device_id=(d, peer),
            device_id_type=MESH,
        )

    for c in range(cuts):

        def y_add(k, z):
            p = order(k)
            y_copy(c, k, p, p, p).wait_recv()
            return z + yrecv[c, p].astype(jnp.float32)

        z = lax.fori_loop(1, chips, y_add, yown[c, chip] + precv[c, chip].astype(jnp.float32))
        for j in range(nt):
            zsend[c, j] = z[:, j * part : (j + 1) * part].astype(zsend.dtype)

        @pl.loop(1, nt)
        def _(k):
            z_copy(c, k, t, lax.rem(t + k, nt), t).start()

    def yz_drain():
        for c in range(cuts):
            pl.loop(1, chips)(lambda k: y_copy(c, k, chip, order(k), chip).wait_send())
            pl.loop(1, nt)(lambda k: z_copy(c, k, t, lax.rem(t + k, nt), t).wait_send())

    drains.append(yz_drain)

    def q_copy(c, k, which, peer_core, peer, slot):
        return pltpu.make_async_remote_copy(
            src_ref=qsend.at[c, peer_core],
            dst_ref=qbuf.at[c, slot],
            send_sem=sq_s.at[c, k, which],
            recv_sem=sq_r.at[c, slot],
            device_id=(2 * chip + peer_core, peer),
            device_id_type=MESH,
        )

    mine = core * nt + t
    for c in range(cuts):

        def z_add(k, total):
            peer = lax.rem(t + k, nt)
            z_copy(c, k, peer, peer, peer).wait_recv()
            return total + zrecv[c, peer].astype(jnp.float32)

        piece = lax.fori_loop(1, nt, z_add, zsend[c, t].astype(jnp.float32))
        for i in range(2):
            qsend[c, i] = piece[i * rows : (i + 1) * rows].astype(jnp.bfloat16)

        @pl.loop(1, nt)
        def _(k):
            peer = lax.rem(t + k, nt)
            q_copy(c, k, 0, core, peer, mine).start()
            q_copy(c, k, 1, 1 - core, peer, mine).start()

        q_copy(c, 0, 1, 1 - core, t, mine).start()
        qbuf[c, mine] = qsend[c, core]

    def q_drain():
        for c in range(cuts):
            q_copy(c, 0, 1, 1 - core, t, mine).wait_send()

            @pl.loop(1, nt)
            def _(k):
                peer = lax.rem(t + k, nt)
                q_copy(c, k, 0, core, peer, mine).wait_send()
                q_copy(c, k, 1, 1 - core, peer, mine).wait_send()

    drains.append(q_drain)

    band = group * rows
    position = t * ctx + lax.broadcasted_iota(jnp.int32, (1, ctx), 1)
    owned = heads * rows
    eye = lax.broadcasted_iota(jnp.int32, (owned, HD), 0) == lax.broadcasted_iota(
        jnp.int32, (owned, HD), 1
    )

    def a_copy(slot, peer, source):
        return pltpu.make_async_remote_copy(
            src_ref=asend.at[peer],
            dst_ref=arecv.at[slot],
            send_sem=sa_s.at[peer],
            recv_sem=sa_r.at[source],
            device_id=(d, peer),
            device_id_type=MESH,
        )

    def s_copy(slot, peer, source):
        return pltpu.make_async_remote_copy(
            src_ref=ssend.at[peer],
            dst_ref=srecv.at[slot],
            send_sem=ss_s.at[peer],
            recv_sem=ss_r.at[source],
            device_id=(d, peer),
            device_id_type=MESH,
        )

    def attend(g, s):
        span = pl.ds(g * band + s, group * steps, stride=seqs)
        q = q_sc[span, :].astype(jnp.bfloat16)
        scores = lax.dot_general(
            q, kv[s, g, :, :HD], (((1,), (1,)), ((), ())), preferred_element_type=jnp.float32
        )
        masked = jnp.where(position < lengths[s], scores * scale, NEG)
        best = jnp.max(masked, axis=-1, keepdims=True)
        weights = jnp.exp(masked - best)
        total = jnp.sum(weights, axis=-1, keepdims=True)
        acc = jnp.dot(
            weights.astype(jnp.bfloat16), kv[s, g, :, HD:], preferred_element_type=jnp.float32
        )
        acc_sc[span, :] = acc
        m_sc[span, :] = jnp.broadcast_to(best, acc.shape)
        l_sc[span, :] = jnp.broadcast_to(total, acc.shape)

    heads_slot = part // HD
    side = kvh // 2 // cuts
    finished = set()
    sent = set()
    for c in range(cuts):
        q_copy(c, 0, 1, 1 - core, t, (1 - core) * nt + t).wait_recv()

        @pl.loop(1, nt)
        def _(k):
            peer = lax.rem(t + k, nt)
            q_copy(c, k, 0, core, peer, core * nt + peer).wait_recv()
            q_copy(c, k, 1, core, peer, (1 - core) * nt + peer).wait_recv()

        for slot in range(2 * nt):
            block = qbuf[c, slot].astype(jnp.float32)
            first = (slot // nt * half + c * wide) // HD + slot % nt * heads_slot
            for j in range(heads_slot):
                h = first + j
                q_sc[h * rows : (h + 1) * rows, :] = block[:, j * HD : (j + 1) * HD]

        ready = [i * (kvh // 2) + c * side + j for i in range(2) for j in range(side)]
        for g in ready:
            for s in range(seqs):
                load_kv[s][g].wait()
        for g in ready:
            for s in range(seqs):
                attend(g, s)
        finished.update(ready)
        for j in range(nt):
            needs = {h // group for h in range(j * heads, (j + 1) * heads)}
            if j in sent or not needs <= finished:
                continue
            sent.add(j)
            window = slice(j * owned, (j + 1) * owned)
            asend[j] = acc_sc[window, :].astype(asend.dtype)
            for i, ref in enumerate((m_sc, l_sc)):
                ssend[j, i : i + 1, :] = jnp.sum(
                    jnp.where(eye, ref[window, :], 0.0), axis=0, keepdims=True
                )

            @pl.when(t != j)
            def _():
                a_copy(t, j, t).start()
                s_copy(t, j, t).start()

    own = pl.ds(pl.multiple_of(t * owned, owned), owned)
    q_own = q_sc[own, :].astype(jnp.bfloat16)
    new_keys = fresh[:, :HD].astype(jnp.bfloat16)
    new_values = fresh[:, HD:].astype(jnp.bfloat16)
    new_scores = (
        lax.dot_general(
            q_own, new_keys, (((1,), (1,)), ((), ())), preferred_element_type=jnp.float32
        )
        * scale
    )
    row = lax.broadcasted_iota(jnp.int32, new_scores.shape, 0)
    col = lax.broadcasted_iota(jnp.int32, new_scores.shape, 1)
    col_row = col // kvh
    causal = (
        (lax.rem(col, kvh) == t * heads // group)
        & (lax.rem(row, seqs) == lax.rem(col_row, seqs))
        & (lax.rem(row, rows) // seqs >= col_row // seqs)
    )
    new_masked = jnp.where(causal, new_scores, NEG)
    top = jnp.max(new_masked, axis=-1, keepdims=True)
    new_weights = jnp.where(causal, jnp.exp(new_masked - top), 0.0)
    denom = jnp.sum(new_weights, axis=-1, keepdims=True)
    accum = jnp.dot(
        new_weights.astype(jnp.bfloat16), new_values, preferred_element_type=jnp.float32
    )

    def join(state, best, total, acc):
        top, denom, accum = state
        peak = jnp.maximum(top, best)
        left = jnp.exp(top - peak)
        right = jnp.exp(best - peak)
        return peak, denom * left + total * right, accum * left + acc * right

    state = join((top, denom, accum), m_sc[own, :][:, :1], l_sc[own, :][:, :1], acc_sc[own, :])

    def a_join(k, state):
        peer = lax.rem(t + k, nt)
        a_copy(peer, peer, peer).wait_recv()
        s_copy(peer, peer, peer).wait_recv()
        stats = srecv[peer]
        best = jnp.sum(jnp.where(eye, stats[0:1, :], 0.0), axis=1, keepdims=True)
        total = jnp.sum(jnp.where(eye, stats[1:2, :], 0.0), axis=1, keepdims=True)
        return join(state, best, total, arecv[peer].astype(jnp.float32))

    top, denom, accum = lax.fori_loop(1, nt, a_join, state)
    result = accum / denom
    for j in range(heads):
        for i in range(steps):
            r = j * rows + i * seqs
            out[i, :, j * HD : (j + 1) * HD] = result[r : r + seqs].astype(out.dtype)

    def a_drain():
        @pl.loop(1, nt)
        def _(k):
            peer = lax.rem(t + k, nt)
            a_copy(t, peer, t).wait_send()
            s_copy(t, peer, t).wait_send()

    drains.append(a_drain)
    for drain in drains:
        drain()


def body(wq_flat, hidden, cache, new_kv, lengths):
    nt = lax.axis_size("tensor")
    n = lax.axis_size("dp")
    t = lax.axis_index("tensor")
    steps, seqs, width = hidden.shape
    rows = steps * seqs
    depth, columns = wq_flat.shape
    kvh, ctx = cache.shape[1], cache.shape[2]
    half = columns // 2
    cuts = 2 if half // (2 * nt) % HD == 0 and kvh % 4 == 0 else 1
    wide = half // cuts
    part = wide // nt
    heads = QH // nt
    owned = heads * rows
    chips = n // 2
    bf16, f32 = jnp.bfloat16, jnp.float32
    dma = pltpu.SemaphoreType.DMA
    vmem = pl.BlockSpec(memory_space=pltpu.VMEM)
    blocked = depth % 128 != 0
    blocks = hidden
    if blocked:
        blocks = hidden.reshape(rows, n, nt, depth)
        blocks = lax.dynamic_index_in_dim(blocks, t, 2, keepdims=False).astype(f32)
        blocks = blocks.transpose(1, 0, 2)
    held = (rows, depth) if blocked else (steps, seqs, depth)
    anywhere = pl.BlockSpec(memory_space=pl.ANY)
    result = pl.pallas_call(
        functools.partial(kernel, n, nt, blocked),
        out_shape=jax.ShapeDtypeStruct((steps, seqs, heads * HD), f32),
        in_specs=[pl.BlockSpec(memory_space=pltpu.SMEM), anywhere, vmem if blocked else anywhere, anywhere, anywhere, anywhere],
        out_specs=vmem,
        scratch_shapes=[
            pltpu.VMEM(hidden.shape, bf16),
            pltpu.VMEM(new_kv.shape, bf16),
            dma((2,)),
            pltpu.VMEM((depth, half), bf16),
            pltpu.VMEM((depth, half), bf16),
            pltpu.VMEM(cache.shape, bf16),
            pltpu.VMEM((rows * kvh, 2 * HD), f32),
            pltpu.VMEM((n * rows, depth), f32),
            pltpu.VMEM((n, *held), blocks.dtype),
            pltpu.VMEM((cuts, chips, 2 * rows, wide), f32),
            pltpu.VMEM((cuts, chips, 2 * rows, wide), bf16),
            pltpu.VMEM((cuts, chips, 2 * rows, wide), bf16),
            pltpu.VMEM((cuts, chips, 2 * rows, wide), bf16),
            pltpu.VMEM((cuts, chips, 2 * rows, wide), bf16),
            pltpu.VMEM((cuts, nt, 2 * rows, part), bf16),
            pltpu.VMEM((cuts, nt, 2 * rows, part), bf16),
            pltpu.VMEM((cuts, 2, rows, part), bf16),
            pltpu.VMEM((cuts, 2 * nt, rows, part), bf16),
            pltpu.VMEM((QH * rows, HD), f32),
            pltpu.VMEM((QH * rows, HD), f32),
            pltpu.VMEM((nt, owned, HD), bf16),
            pltpu.VMEM((nt, owned, HD), bf16),
            pltpu.VMEM((QH * rows, HD), f32),
            pltpu.VMEM((QH * rows, HD), f32),
            pltpu.VMEM((nt, 8, HD), f32),
            pltpu.VMEM((nt, 8, HD), f32),
            dma((2,)),
            dma((seqs, kvh)),
            dma((n,)),
            dma((n,)),
            dma((cuts, chips)),
            dma((cuts, chips)),
            dma((cuts, chips)),
            dma((cuts, chips)),
            dma((cuts, nt)),
            dma((cuts, nt)),
            dma((cuts, nt, 2)),
            dma((cuts, 2 * nt)),
            dma((nt,)),
            dma((nt,)),
            dma((nt,)),
            dma((nt,)),
        ],
        compiler_params=pltpu.CompilerParams(collective_id=0, has_side_effects=True),
    )(lengths, hidden, blocks, new_kv, wq_flat, cache)
    return result.astype(bf16)


def solution(mesh):
    placed = (
        P(("dp", "tensor"), None),
        P(None, "dp", None),
        P("dp", None, "tensor", None),
        P(None, "dp", None, None),
        P("dp"),
    )
    return jax.shard_map(
        body, mesh=mesh, in_specs=placed, out_specs=P(None, "dp", "tensor"), check_vma=False
    )
```

```python
import functools

import jax
import jax.numpy as jnp
from jax import lax
from jax.experimental import pallas as pl
from jax.experimental.pallas import tpu as pltpu
from jax.sharding import PartitionSpec as P

QH = 32
HD = 128
MESH = pl.DeviceIdType.MESH
NEG = -1e30


def kernel(
    n,
    nt,
    blocked,
    lengths,
    hid_any,
    blocks,
    new_any,
    wq,
    cache,
    out,
    hid,
    new_kv,
    sem_in,
    wq_own,
    wq_other,
    kv,
    fresh,
    x_sc,
    xg,
    yown,
    ysend,
    yrecv,
    psend,
    precv,
    zsend,
    zrecv,
    qsend,
    qbuf,
    q_sc,
    acc_sc,
    asend,
    arecv,
    m_sc,
    l_sc,
    ssend,
    srecv,
    sem_w,
    sem_kv,
    sx_s,
    sx_r,
    sy_s,
    sy_r,
    sp_s,
    sp_r,
    sz_s,
    sz_r,
    sq_s,
    sq_r,
    sa_s,
    sa_r,
    ss_s,
    ss_r,
):
    d = lax.axis_index("dp")
    t = lax.axis_index("tensor")
    core = lax.rem(d, 2)
    chip = d // 2
    chips = n // 2
    mate = d + 1 - 2 * core
    steps, seqs, width = hid.shape
    depth = wq_own.shape[0]
    rows = steps * seqs
    half = wq_own.shape[1]
    _, kvh, ctx, _ = kv.shape
    drains = []
    heads = QH // nt
    group = QH // kvh
    scale = 1.0 / HD**0.5

    load_hid = pltpu.make_async_copy(hid_any, hid, sem_in.at[0])
    load_new = pltpu.make_async_copy(new_any, new_kv, sem_in.at[1])
    load_hid.start()
    load_new.start()
    load_other = pltpu.make_async_copy(
        wq.at[:, pl.ds(pl.multiple_of((1 - core) * half, half), half)], wq_other, sem_w.at[0]
    )
    load_own = pltpu.make_async_copy(
        wq.at[:, pl.ds(pl.multiple_of(core * half, half), half)], wq_own, sem_w.at[1]
    )
    load_other.start()
    load_own.start()
    load_kv = [
        [pltpu.make_async_copy(cache.at[s, g], kv.at[s, g], sem_kv.at[s, g]) for g in range(kvh)]
        for s in range(seqs)
    ]
    for g in range(kvh):
        for s in range(seqs):
            load_kv[s][g].start()

    barrier = pltpu.get_barrier_semaphore()

    @pl.loop(1, n)
    def _(k):
        pl.semaphore_signal(
            barrier, inc=1, device_id=(lax.rem(d + k, n), t), device_id_type=MESH
        )

    @pl.loop(1, nt)
    def _(k):
        peer = lax.rem(t + k, nt)
        pl.semaphore_signal(barrier, inc=1, device_id=(d, peer), device_id_type=MESH)
        pl.semaphore_signal(barrier, inc=1, device_id=(mate, peer), device_id_type=MESH)

    pl.semaphore_wait(barrier, n - 1 + 2 * (nt - 1))

    load_hid.wait()
    load_new.wait()

    def columns_of(peer):
        if blocked:
            return blocks.at[peer]
        start = pl.multiple_of((peer * nt + t) * depth, depth)
        return hid.at[:, :, pl.ds(start, depth)]

    def x_copy(k, slot, peer, source):
        return pltpu.make_async_remote_copy(
            src_ref=columns_of(peer),
            dst_ref=xg.at[slot],
            send_sem=sx_s.at[k],
            recv_sem=sx_r.at[source],
            device_id=(peer, t),
            device_id_type=MESH,
        )

    @pl.loop(1, n)
    def _(k):
        x_copy(k, d, lax.rem(d + k, n), d).start()

    xg[d] = columns_of(d)[...]
    for i in range(steps):
        for s in range(seqs):
            r = (i * seqs + s) * kvh
            fresh[r : r + kvh, :] = new_kv[i, s].astype(jnp.float32)
    load_other.wait()
    load_own.wait()

    @pl.loop(1, n)
    def _(k):
        peer = lax.rem(d + k, n)
        x_copy(k, peer, peer, peer).wait_recv()

    drains.append(lambda: pl.loop(1, n)(lambda k: x_copy(k, d, lax.rem(d + k, n), d).wait_send()))
    if blocked:
        x = xg[...].reshape(n * rows, depth).astype(jnp.bfloat16)
    else:
        for p in range(n):
            for i in range(steps):
                r = p * rows + i * seqs
                x_sc[r : r + seqs, :] = xg[p, i].astype(jnp.float32)
        x = x_sc[...].astype(jnp.bfloat16)

    cuts = psend.shape[0]
    wide = half // cuts

    def p_copy(c, p):
        return pltpu.make_async_remote_copy(
            src_ref=psend.at[c, p],
            dst_ref=precv.at[c, p],
            send_sem=sp_s.at[c, p],
            recv_sem=sp_r.at[c, p],
            device_id=(mate, t),
            device_id_type=MESH,
        )

    def order(k):
        return lax.rem(chip + chips - k, chips)

    for c in range(cuts):
        psend[c] = (
            jnp.dot(
                x, wq_other[:, c * wide : (c + 1) * wide], preferred_element_type=jnp.float32
            )
            .astype(jnp.bfloat16)
            .reshape(chips, 2 * rows, wide)
        )

        @pl.loop(1, chips + 1)
        def _(k):
            p_copy(c, order(k)).start()

    for c in range(cuts):
        yown[c] = jnp.dot(
            x, wq_own[:, c * wide : (c + 1) * wide], preferred_element_type=jnp.float32
        ).reshape(chips, 2 * rows, wide)

    def p_drain():
        for c in range(cuts):
            pl.loop(1, chips + 1)(lambda k: p_copy(c, order(k)).wait_send())

    drains.append(p_drain)

    def y_copy(c, k, slot, peer, source):
        return pltpu.make_async_remote_copy(
            src_ref=ysend.at[c, peer],
            dst_ref=yrecv.at[c, slot],
            send_sem=sy_s.at[c, k],
            recv_sem=sy_r.at[c, source],
            device_id=(2 * peer + core, t),
            device_id_type=MESH,
        )

    for c in range(cuts):

        @pl.loop(1, chips)
        def _(k):
            p = order(k)
            p_copy(c, p).wait_recv()
            ysend[c, p] = (yown[c, p] + precv[c, p].astype(jnp.float32)).astype(jnp.bfloat16)
            y_copy(c, k, chip, p, chip).start()

        p_copy(c, chip).wait_recv()

    part = wide // nt

    def z_copy(c, k, slot, peer, source):
        return pltpu.make_async_remote_copy(
            src_ref=zsend.at[c, peer],
            dst_ref=zrecv.at[c, slot],
            send_sem=sz_s.at[c, k],
            recv_sem=sz_r.at[c, source],
            device_id=(d, peer),
            device_id_type=MESH,
        )

    for c in range(cuts):

        def y_add(k, z):
            p = order(k)
            y_copy(c, k, p, p, p).wait_recv()
            return z + yrecv[c, p].astype(jnp.float32)

        z = lax.fori_loop(1, chips, y_add, yown[c, chip] + precv[c, chip].astype(jnp.float32))
        for j in range(nt):
            zsend[c, j] = z[:, j * part : (j + 1) * part].astype(zsend.dtype)

        @pl.loop(1, nt)
        def _(k):
            z_copy(c, k, t, lax.rem(t + k, nt), t).start()

    def yz_drain():
        for c in range(cuts):
            pl.loop(1, chips)(lambda k: y_copy(c, k, chip, order(k), chip).wait_send())
            pl.loop(1, nt)(lambda k: z_copy(c, k, t, lax.rem(t + k, nt), t).wait_send())

    drains.append(yz_drain)

    def q_copy(c, k, which, peer_core, peer, slot):
        return pltpu.make_async_remote_copy(
            src_ref=qsend.at[c, peer_core],
            dst_ref=qbuf.at[c, slot],
            send_sem=sq_s.at[c, k, which],
            recv_sem=sq_r.at[c, slot],
            device_id=(2 * chip + peer_core, peer),
            device_id_type=MESH,
        )

    mine = core * nt + t
    for c in range(cuts):

        def z_add(k, total):
            peer = lax.rem(t + k, nt)
            z_copy(c, k, peer, peer, peer).wait_recv()
            return total + zrecv[c, peer].astype(jnp.float32)

        piece = lax.fori_loop(1, nt, z_add, zsend[c, t].astype(jnp.float32))
        for i in range(2):
            qsend[c, i] = piece[i * rows : (i + 1) * rows].astype(jnp.bfloat16)

        @pl.loop(1, nt)
        def _(k):
            peer = lax.rem(t + k, nt)
            q_copy(c, k, 0, core, peer, mine).start()
            q_copy(c, k, 1, 1 - core, peer, mine).start()

        q_copy(c, 0, 1, 1 - core, t, mine).start()
        qbuf[c, mine] = qsend[c, core]

    def q_drain():
        for c in range(cuts):
            q_copy(c, 0, 1, 1 - core, t, mine).wait_send()

            @pl.loop(1, nt)
            def _(k):
                peer = lax.rem(t + k, nt)
                q_copy(c, k, 0, core, peer, mine).wait_send()
                q_copy(c, k, 1, 1 - core, peer, mine).wait_send()

    drains.append(q_drain)

    band = group * rows
    position = t * ctx + lax.broadcasted_iota(jnp.int32, (1, ctx), 1)
    owned = heads * rows
    eye = lax.broadcasted_iota(jnp.int32, (owned, HD), 0) == lax.broadcasted_iota(
        jnp.int32, (owned, HD), 1
    )

    def a_copy(slot, peer, source):
        return pltpu.make_async_remote_copy(
            src_ref=asend.at[peer],
            dst_ref=arecv.at[slot],
            send_sem=sa_s.at[peer],
            recv_sem=sa_r.at[source],
            device_id=(d, peer),
            device_id_type=MESH,
        )

    def s_copy(slot, peer, source):
        return pltpu.make_async_remote_copy(
            src_ref=ssend.at[peer],
            dst_ref=srecv.at[slot],
            send_sem=ss_s.at[peer],
            recv_sem=ss_r.at[source],
            device_id=(d, peer),
            device_id_type=MESH,
        )

    def attend(g, s):
        base = pl.ds(pl.multiple_of(g * band, band), band)
        span = pl.ds(s, group * steps, stride=seqs)
        q = q_sc.at[base][span, :].astype(jnp.bfloat16)
        scores = lax.dot_general(
            q, kv[s, g, :, :HD], (((1,), (1,)), ((), ())), preferred_element_type=jnp.float32
        )
        masked = jnp.where(position < lengths[s], scores * scale, NEG)
        best = jnp.max(masked, axis=-1, keepdims=True)
        weights = jnp.exp(masked - best)
        total = jnp.sum(weights, axis=-1, keepdims=True)
        acc = jnp.dot(
            weights.astype(jnp.bfloat16), kv[s, g, :, HD:], preferred_element_type=jnp.float32
        )
        acc_sc.at[base][span, :] = acc
        m_sc.at[base][span, :] = jnp.broadcast_to(best, acc.shape)
        l_sc.at[base][span, :] = jnp.broadcast_to(total, acc.shape)

    heads_slot = part // HD
    side = kvh // 2 // cuts
    per = group // heads
    far = (2 * t < nt).astype(jnp.int32)
    for c in range(cuts):
        q_copy(c, 0, 1, 1 - core, t, (1 - core) * nt + t).wait_recv()

        @pl.loop(1, nt)
        def _(k):
            peer = lax.rem(t + k, nt)
            q_copy(c, k, 0, core, peer, core * nt + peer).wait_recv()
            q_copy(c, k, 1, core, peer, (1 - core) * nt + peer).wait_recv()

        for slot in range(2 * nt):
            block = qbuf[c, slot].astype(jnp.float32)
            first = (slot // nt * half + c * wide) // HD + slot % nt * heads_slot
            for j in range(heads_slot):
                h = first + j
                q_sc[h * rows : (h + 1) * rows, :] = block[:, j * HD : (j + 1) * HD]

        ready = [i * (kvh // 2) + c * side + j for i in range(2) for j in range(side)]
        for g in ready:
            for s in range(seqs):
                load_kv[s][g].wait()
        for low, high in zip(ready, ready[::-1]):
            g = low + (high - low) * far
            for s in range(seqs):
                attend(g, s)
            for i in range(per):
                j = g * per + i
                window = pl.ds(pl.multiple_of(j * owned, owned), owned)
                asend[j] = acc_sc[window, :].astype(asend.dtype)
                for at, ref in enumerate((m_sc, l_sc)):
                    ssend[j, at : at + 1, :] = jnp.sum(
                        jnp.where(eye, ref[window, :], 0.0), axis=0, keepdims=True
                    )

                @pl.when(t != j)
                def _():
                    a_copy(t, j, t).start()
                    s_copy(t, j, t).start()

    own = pl.ds(pl.multiple_of(t * owned, owned), owned)
    q_own = q_sc[own, :].astype(jnp.bfloat16)
    new_keys = fresh[:, :HD].astype(jnp.bfloat16)
    new_values = fresh[:, HD:].astype(jnp.bfloat16)
    new_scores = (
        lax.dot_general(
            q_own, new_keys, (((1,), (1,)), ((), ())), preferred_element_type=jnp.float32
        )
        * scale
    )
    row = lax.broadcasted_iota(jnp.int32, new_scores.shape, 0)
    col = lax.broadcasted_iota(jnp.int32, new_scores.shape, 1)
    col_row = col // kvh
    causal = (
        (lax.rem(col, kvh) == t * heads // group)
        & (lax.rem(row, seqs) == lax.rem(col_row, seqs))
        & (lax.rem(row, rows) // seqs >= col_row // seqs)
    )
    new_masked = jnp.where(causal, new_scores, NEG)
    top = jnp.max(new_masked, axis=-1, keepdims=True)
    new_weights = jnp.where(causal, jnp.exp(new_masked - top), 0.0)
    denom = jnp.sum(new_weights, axis=-1, keepdims=True)
    accum = jnp.dot(
        new_weights.astype(jnp.bfloat16), new_values, preferred_element_type=jnp.float32
    )

    def join(state, best, total, acc):
        top, denom, accum = state
        peak = jnp.maximum(top, best)
        left = jnp.exp(top - peak)
        right = jnp.exp(best - peak)
        return peak, denom * left + total * right, accum * left + acc * right

    state = join((top, denom, accum), m_sc[own, :][:, :1], l_sc[own, :][:, :1], acc_sc[own, :])

    def a_join(k, state):
        peer = lax.rem(t + k, nt)
        a_copy(peer, peer, peer).wait_recv()
        s_copy(peer, peer, peer).wait_recv()
        stats = srecv[peer]
        best = jnp.sum(jnp.where(eye, stats[0:1, :], 0.0), axis=1, keepdims=True)
        total = jnp.sum(jnp.where(eye, stats[1:2, :], 0.0), axis=1, keepdims=True)
        return join(state, best, total, arecv[peer].astype(jnp.float32))

    top, denom, accum = lax.fori_loop(1, nt, a_join, state)
    result = accum / denom
    for j in range(heads):
        for i in range(steps):
            r = j * rows + i * seqs
            out[i, :, j * HD : (j + 1) * HD] = result[r : r + seqs].astype(out.dtype)

    def a_drain():
        @pl.loop(1, nt)
        def _(k):
            peer = lax.rem(t + k, nt)
            a_copy(t, peer, t).wait_send()
            s_copy(t, peer, t).wait_send()

    drains.append(a_drain)
    for drain in drains:
        drain()


def body(wq_flat, hidden, cache, new_kv, lengths):
    nt = lax.axis_size("tensor")
    n = lax.axis_size("dp")
    t = lax.axis_index("tensor")
    steps, seqs, width = hidden.shape
    rows = steps * seqs
    depth, columns = wq_flat.shape
    kvh, ctx = cache.shape[1], cache.shape[2]
    half = columns // 2
    cuts = 2 if half // (2 * nt) % HD == 0 and kvh % 4 == 0 else 1
    wide = half // cuts
    part = wide // nt
    heads = QH // nt
    owned = heads * rows
    chips = n // 2
    bf16, f32 = jnp.bfloat16, jnp.float32
    dma = pltpu.SemaphoreType.DMA
    vmem = pl.BlockSpec(memory_space=pltpu.VMEM)
    blocked = depth % 128 != 0
    blocks = hidden
    if blocked:
        blocks = hidden.reshape(rows, n, nt, depth)
        blocks = lax.dynamic_index_in_dim(blocks, t, 2, keepdims=False).astype(f32)
        blocks = blocks.transpose(1, 0, 2)
    held = (rows, depth) if blocked else (steps, seqs, depth)
    anywhere = pl.BlockSpec(memory_space=pl.ANY)
    result = pl.pallas_call(
        functools.partial(kernel, n, nt, blocked),
        out_shape=pltpu.VMEM((steps, seqs, heads * HD), f32),
        in_specs=[pl.BlockSpec(memory_space=pltpu.SMEM), anywhere, vmem if blocked else anywhere, anywhere, anywhere, anywhere],
        out_specs=vmem,
        scratch_shapes=[
            pltpu.VMEM(hidden.shape, bf16),
            pltpu.VMEM(new_kv.shape, bf16),
            dma((2,)),
            pltpu.VMEM((depth, half), bf16),
            pltpu.VMEM((depth, half), bf16),
            pltpu.VMEM(cache.shape, bf16),
            pltpu.VMEM((rows * kvh, 2 * HD), f32),
            pltpu.VMEM((n * rows, depth), f32),
            pltpu.VMEM((n, *held), blocks.dtype),
            pltpu.VMEM((cuts, chips, 2 * rows, wide), f32),
            pltpu.VMEM((cuts, chips, 2 * rows, wide), bf16),
            pltpu.VMEM((cuts, chips, 2 * rows, wide), bf16),
            pltpu.VMEM((cuts, chips, 2 * rows, wide), bf16),
            pltpu.VMEM((cuts, chips, 2 * rows, wide), bf16),
            pltpu.VMEM((cuts, nt, 2 * rows, part), bf16),
            pltpu.VMEM((cuts, nt, 2 * rows, part), bf16),
            pltpu.VMEM((cuts, 2, rows, part), bf16),
            pltpu.VMEM((cuts, 2 * nt, rows, part), bf16),
            pltpu.VMEM((QH * rows, HD), f32),
            pltpu.VMEM((QH * rows, HD), f32),
            pltpu.VMEM((nt, owned, HD), bf16),
            pltpu.VMEM((nt, owned, HD), bf16),
            pltpu.VMEM((QH * rows, HD), f32),
            pltpu.VMEM((QH * rows, HD), f32),
            pltpu.VMEM((nt, 8, HD), f32),
            pltpu.VMEM((nt, 8, HD), f32),
            dma((2,)),
            dma((seqs, kvh)),
            dma((n,)),
            dma((n,)),
            dma((cuts, chips)),
            dma((cuts, chips)),
            dma((cuts, chips)),
            dma((cuts, chips)),
            dma((cuts, nt)),
            dma((cuts, nt)),
            dma((cuts, nt, 2)),
            dma((cuts, 2 * nt)),
            dma((nt,)),
            dma((nt,)),
            dma((nt,)),
            dma((nt,)),
        ],
        compiler_params=pltpu.CompilerParams(collective_id=0, has_side_effects=True),
    )(lengths, hidden, blocks, new_kv, wq_flat, cache)
    return result.astype(bf16)


def solution(mesh):
    placed = (
        P(("dp", "tensor"), None),
        P(None, "dp", None),
        P("dp", None, "tensor", None),
        P(None, "dp", None, None),
        P("dp"),
    )
    return jax.shard_map(
        body, mesh=mesh, in_specs=placed, out_specs=P(None, "dp", "tensor"), check_vma=False
    )
```
